32 devices in a mesh: rep: 2 (over x), ctx: 16 (over z, y, core).
Axes of the slice: x: 2, y: 2, z: 4, core: 2. Of those that a mesh axis runs over, the one named last changes fastest.
Arguments:
- queries: bfloat16 [4096, 12288], P(('rep', 'ctx')), parts along dimension 0, may hold values from -8 to 8
- latents: bfloat16 [512, 576], P(('rep', 'ctx')), parts along dimension 0, may hold values from -8 to 8
- w_key: bfloat16 [64, 512, 128], P('ctx'), may hold values from -0.25 to 0.25
- w_value: bfloat16 [64, 512, 128], P('ctx'), may hold values from -0.25 to 0.25
Outputs:
- attended: bfloat16 [4096, 8192], P(('rep', 'ctx')), parts along dimension 0
The draws below stay inside these ranges and needn't reach their ends.
There are 2 independent parts, one for each index of `rep`. The reference program is written for one: setup_inputs(seed, part) draws one part's arguments, and reference() takes and returns one part's arrays. A program takes and returns all parts, laid end to end along the dimension named above; an argument that names none is the same for every part. Nothing has to cross between parts.
All inputs are finite; a program needn't handle non-finite values.
Results may differ from the reference program's by a relative error of at most 0.0067.
Values may be sent and summed in bfloat16 or wider, within the bound.
A program may use at most 128 MiB of HBM per device.

```python
import jax
import jax.numpy as jnp
from jax import lax

DLAT = 512
DROPE = 64
DNOPE = 128
DV = 128
H = 64
QUERIES = 2048
CACHE = 256


def draw_queries(key, part):
    qk_width = DNOPE + DROPE
    value_key = jax.random.fold_in(key, 11)
    values_all = jnp.clip(2.5 * jax.random.normal(value_key, (QUERIES, H, qk_width), jnp.float32), -8.0, 8.0)
    return values_all.reshape(QUERIES, H * qk_width).astype(jnp.bfloat16)


def draw_latents(key, part):
    value_key = jax.random.fold_in(key, 12)
    values_all = jnp.clip(jax.random.normal(value_key, (CACHE, DLAT + DROPE), jnp.float32), -8.0, 8.0)
    return values_all.astype(jnp.bfloat16)


def block_levels(rng, dims, cuts, smallest, top_value):
    factor_of = 1.0
    for position, blocks in cuts:
        steps = jax.random.uniform(jax.random.fold_in(jax.random.fold_in(rng, 6), position), (blocks,), jnp.float32, smallest / len(cuts), top_value / len(cuts))
        factor_of = factor_of * jnp.repeat(jnp.exp(steps), dims[position] // blocks).reshape((-1,) + (1,) * (len(dims) - 1 - position))
    return factor_of


def scatter_about(own_key, shape, width, reach, pieces=(), held_as=jnp.bfloat16):
    entries = width * jax.random.normal(own_key, shape, jnp.float32)
    if pieces:
        entries = entries * block_levels(own_key, shape, pieces, -0.22, 0.18)
    return jnp.clip(entries, -reach, reach).astype(held_as)


def setup_inputs(seed: int = 0, part: int = 0) -> dict:
    arg_keys = jax.random.split(jax.random.key(seed), 5)
    own_keys = jax.random.split(jax.random.fold_in(arg_keys[4], part), 5)
    return {
        "queries": draw_queries(jax.random.fold_in(jax.random.fold_in(arg_keys[4], part), 71), part),
        "latents": draw_latents(jax.random.fold_in(jax.random.fold_in(arg_keys[4], part), 71), part),
        "w_key": scatter_about(arg_keys[2], (H, DLAT, DNOPE), DLAT ** -0.5, 0.25, ((0, 16),)),
        "w_value": scatter_about(arg_keys[3], (H, DLAT, DV), DLAT ** -0.5, 0.25, ((0, 16),)),
    }


def reference(queries, latents, w_key, w_value):
    query_count = queries.shape[0]
    qk_width = DNOPE + DROPE
    shaped = queries.reshape(query_count, H, qk_width)
    latent_part = latents[:, :DLAT].astype(jnp.float32)
    rope_part = latents[:, DLAT:]
    score_scale = 1.0 / (qk_width ** 0.5)

    def per_head(head_index):
        key_proj = w_key[head_index].astype(jnp.float32)
        value_proj = w_value[head_index].astype(jnp.float32)
        keys_nope = jnp.dot(latent_part, key_proj).astype(jnp.bfloat16)
        values_head = jnp.dot(latent_part, value_proj).astype(jnp.bfloat16)
        keys_nope = lax.optimization_barrier(keys_nope)
        values_head = lax.optimization_barrier(values_head)
        keys_full = jnp.concatenate([keys_nope, rope_part], axis=1).astype(jnp.float32)
        query_head = shaped[:, head_index, :].astype(jnp.float32)
        scores = jnp.dot(query_head, keys_full.T) * score_scale
        row_max = jnp.max(scores, axis=1)
        weights = jnp.exp(scores - row_max[:, None])
        total = jnp.sum(weights, axis=1)
        rounded = lax.optimization_barrier(weights.astype(jnp.bfloat16))
        mixed = jnp.dot(rounded.astype(jnp.float32), values_head.astype(jnp.float32))
        return (mixed / total[:, None]).astype(jnp.bfloat16)

    per_heads = lax.map(per_head, jnp.arange(H, dtype=jnp.int32))
    return jnp.transpose(per_heads, (1, 0, 2)).reshape(query_count, H * DV)
```

```python
import functools
import math

import jax
import jax.numpy as jnp
from jax import lax
from jax.experimental import pallas as pl
from jax.experimental.pallas import tpu as pltpu
from jax.sharding import PartitionSpec as P

MESH = pl.DeviceIdType.MESH


def kernel(
    grid_y,
    cores,
    q_hbm,
    lat_hbm,
    wk_hbm,
    wv_hbm,
    out_hbm,
    q,
    lat,
    wkv,
    ropes,
    kv,
    o,
    load_sem,
    out_sem,
    lat_recv,
    lat_send,
    lat_relay,
    kv_recv,
    kv_right,
    kv_left,
    kv_across,
):
    devices = kv.shape[0]
    heads = kv.shape[1]
    rows = kv.shape[3]
    nope = kv.shape[4]
    block = lat.shape[1]
    width = wkv.shape[1]
    rope = lat.shape[2] - width
    qk = nope + rope
    chips = devices // cores
    grid_z = chips // grid_y
    half = chips // 2
    scale = math.log2(math.e) / math.sqrt(qk)

    me = lax.axis_index("ctx")
    core = lax.rem(me, cores)
    my_chip = me // cores
    my_y = lax.rem(my_chip, grid_y)
    my_z = my_chip // grid_y
    place = (1 - my_y) * my_z + my_y * (2 * grid_z - 1 - my_z)

    def device_at(spot, which):
        spot = lax.rem(spot + 2 * chips, chips)
        y = spot // grid_z
        z = (1 - y) * spot + y * (2 * grid_z - 1 - spot)
        return (z * grid_y + y) * cores + which

    other_core = cores - 1 - core
    across = my_chip * cores + other_core
    right = device_at(place + 1, core)
    left = device_at(place - 1, core)

    q_copy = pltpu.make_async_copy(q_hbm, q, load_sem.at[0])
    lat_copy = pltpu.make_async_copy(lat_hbm, lat.at[me], load_sem.at[1])
    lat_copy.start()
    w_copies = []
    for j in range(heads):
        w_copies.append(
            pltpu.make_async_copy(wk_hbm.at[j], wkv.at[j, :, pl.ds(0, nope)], load_sem.at[2 + 2 * j])
        )
        w_copies.append(
            pltpu.make_async_copy(wv_hbm.at[j], wkv.at[j, :, pl.ds(nope, nope)], load_sem.at[3 + 2 * j])
        )
    for copy in w_copies:
        copy.start()
    q_copy.start()

    barrier = pltpu.get_barrier_semaphore()

    @pl.loop(1, chips)
    def _(d):
        pl.semaphore_signal(
            barrier, inc=1, device_id={"ctx": device_at(place + d, core)}, device_id_type=MESH
        )

    pl.semaphore_signal(barrier, inc=1, device_id={"ctx": across}, device_id_type=MESH)
    pl.semaphore_wait(barrier, chips)

    def lat_out(d):
        return pltpu.make_async_remote_copy(
            src_ref=lat_hbm,
            dst_ref=lat.at[me],
            send_sem=lat_send.at[d],
            recv_sem=lat_recv.at[me],
            device_id={"ctx": device_at(place + d, core)},
            device_id_type=MESH,
        )

    def lat_on(owner):
        return pltpu.make_async_remote_copy(
            src_ref=lat.at[owner],
            dst_ref=lat.at[owner],
            send_sem=lat_relay.at[owner],
            recv_sem=lat_recv.at[owner],
            device_id={"ctx": across},
            device_id_type=MESH,
        )

    @pl.loop(1, chips)
    def _(d):
        lat_out(chips - d).start()

    lat_copy.wait()
    lat_on(me).start()

    @pl.loop(1, chips)
    def _(d):
        owner = device_at(place + d, core)
        lat_on(owner).wait_recv()
        lat_on(owner).start()

    @pl.loop(0, chips)
    def _(d):
        lat_on(device_at(place + d, other_core)).wait_recv()

    for copy in w_copies:
        copy.wait()

    lat_all = lat[...].reshape(rows, lat.shape[2])
    rope_part = lat_all[:, width:]
    blank = jnp.zeros_like(rope_part)
    ropes[0] = jnp.concatenate([rope_part, blank], axis=1)
    ropes[1] = jnp.concatenate([blank, rope_part], axis=1)

    def parity(owner, j):
        if heads % 2 == 0:
            return j % 2
        return lax.rem(owner * heads + j, 2)

    def send(owner, j, sems, target):
        return pltpu.make_async_remote_copy(
            src_ref=kv.at[owner, j],
            dst_ref=kv.at[owner, j],
            send_sem=sems.at[owner, j],
            recv_sem=kv_recv.at[owner, j],
            device_id={"ctx": target},
            device_id_type=MESH,
        )

    def go_right(owner, j):
        return send(owner, j, kv_right, right)

    def go_left(owner, j):
        return send(owner, j, kv_left, left)

    def go_across(owner, j):
        return send(owner, j, kv_across, across)

    half_right = (heads + 1) // 2
    for j in range(heads + 1):
        if j < heads:
            both = jnp.dot(lat_all[:, :width], wkv[j], preferred_element_type=jnp.float32)
            keys = both[:, :nope]
            odd = parity(me, j)
            turned = jnp.concatenate([keys[:, rope:], keys[:, :rope]], axis=1)
            if isinstance(odd, int):
                keys = turned if odd else keys
            else:
                keys = jnp.where(odd == 1, turned, keys)
            kv[me, j, 0] = keys.astype(jnp.bfloat16)
            kv[me, j, 1] = both[:, nope:].astype(jnp.bfloat16)
        if j > 0:
            go_right(me, j - 1).start()
            go_left(me, j - 1).start()
            go_across(me, j - 1).start()

    q_copy.wait()

    lane = lax.broadcasted_iota(jnp.int32, (rows, nope), 1)
    upper = lane >= rope

    def attend(owner, j):
        odd = parity(owner, j)
        head = owner * heads + j
        pair = owner * (heads // 2) + j // 2 if heads % 2 == 0 else head // 2
        start = pl.multiple_of(pair * (2 * qk) + odd * nope, nope)
        queries = q[:, pl.ds(start, 2 * nope)]
        keys = kv[owner, j, 0]

        def even_keys():
            return jnp.concatenate([keys, ropes[0]], axis=1)

        def odd_keys():
            return jnp.concatenate(
                [jnp.where(upper, keys, jnp.zeros_like(keys)), jnp.where(upper, ropes[1], keys)], axis=1
            )

        if isinstance(odd, int):
            keys_full = odd_keys() if odd else even_keys()
        else:
            keys_full = jnp.where(odd == 1, odd_keys(), even_keys())
        scores = lax.dot_general(
            queries, keys_full, (((1,), (1,)), ((), ())), preferred_element_type=jnp.float32
        )
        row_max = jnp.max(scores, axis=1, keepdims=True)
        weights = jnp.exp2((scores - row_max) * scale)
        total = jnp.sum(weights, axis=1, keepdims=True)
        mixed = jnp.dot(weights.astype(jnp.bfloat16), kv[owner, j, 1], preferred_element_type=jnp.float32)
        o[:, pl.ds(pl.multiple_of(head * nope, nope), nope)] = (mixed * (1.0 / total)).astype(jnp.bfloat16)

    def put(owner):
        columns = pl.ds(pl.multiple_of(owner * (heads * nope), nope), heads * nope)
        return pltpu.make_async_copy(o.at[:, columns], out_hbm.at[:, columns], out_sem.at[owner])

    def attend_other(owners, js):
        for j in js:
            for owner in owners:
                go_across(owner, j).wait_recv()
            for owner in owners:
                attend(owner, j)
        for owner in owners:
            put(owner).start()

    for j in range(heads):
        attend(me, j)
    put(me).start()

    def ring_step(s, fwd_right, fwd_left, before):
        from_left = device_at(place - s, core)
        from_right = device_at(place + s, core)
        for j in range(heads):
            go_right(from_left, j).wait_recv()
            if j < fwd_right:
                go_right(from_left, j).start()
            go_across(from_left, j).start()
            go_left(from_right, j).wait_recv()
            if j >= fwd_left:
                go_left(from_right, j).start()
            go_across(from_right, j).start()
            for owner in before:
                go_across(owner, j).wait_recv()
            attend(from_left, j)
            attend(from_right, j)
            for owner in before:
                attend(owner, j)
        put(from_left).start()
        put(from_right).start()
        for owner in before:
            put(owner).start()

    def others(s):
        return (device_at(place - s, other_core), device_at(place + s, other_core))

    if half > 1:
        first_right = heads if half > 2 else half_right
        first_left = 0 if half > 2 else half_right
        ring_step(1, first_right, first_left, (across,))
        if half > 3:

            @pl.loop(2, half - 1)
            def _(s):
                ring_step(s, heads, 0, others(s - 1))

        if half > 2:
            ring_step(half - 1, half_right, half_right, others(half - 2))

    far = device_at(place + half, core)
    far_other = device_at(place + half, other_core)
    last_before = others(half - 1) if half > 1 else (across,)
    order = []
    for j in range(half_right):
        order.append(j)
        if j + half_right < heads:
            order.append(j + half_right)
    for j in order:
        (go_right if j < half_right else go_left)(far, j).wait_recv()
        go_across(far, j).start()
        for owner in last_before:
            go_across(owner, j).wait_recv()
        for owner in last_before:
            attend(owner, j)
        attend(far, j)
    for owner in last_before:
        put(owner).start()
    put(far).start()
    attend_other((far_other,), order)

    @pl.loop(1, chips)
    def _(d):
        lat_out(d).wait_send()

    @pl.loop(0, chips)
    def _(d):
        owner = device_at(place + d, core)
        lat_on(owner).wait_send()
        for j in range(heads):
            go_across(owner, j).wait_send()

    @pl.loop(0, half - 1)
    def _(s):
        for j in range(heads):
            go_right(device_at(place - s, core), j).wait_send()
            go_left(device_at(place + s, core), j).wait_send()

    for j in range(heads):
        if j < half_right:
            go_right(device_at(place - (half - 1), core), j).wait_send()
        else:
            go_left(device_at(place + (half - 1), core), j).wait_send()

    @pl.loop(0, devices)
    def _(owner):
        put(owner).wait()


def on_device(grid_y, cores, queries, latents, w_key, w_value):
    devices = lax.axis_size("ctx")
    heads, width, nope = w_key.shape
    query_rows = queries.shape[0]
    block = latents.shape[0]
    rows = block * devices
    chips = devices // cores
    anywhere = pl.BlockSpec(memory_space=pl.ANY)
    dma = pltpu.SemaphoreType.DMA
    return pl.pallas_call(
        functools.partial(kernel, grid_y, cores),
        out_shape=jax.ShapeDtypeStruct((query_rows, devices * heads * nope), jnp.bfloat16),
        in_specs=[anywhere] * 4,
        out_specs=anywhere,
        scratch_shapes=[
            pltpu.VMEM(queries.shape, jnp.bfloat16),
            pltpu.VMEM((devices, block, latents.shape[1]), jnp.bfloat16),
            pltpu.VMEM((heads, width, 2 * nope), jnp.bfloat16),
            pltpu.VMEM((2, rows, nope), jnp.bfloat16),
            pltpu.VMEM((devices, heads, 2, rows, nope), jnp.bfloat16),
            pltpu.VMEM((query_rows, devices * heads * nope), jnp.bfloat16),
            dma((2 + 2 * heads,)),
            dma((devices,)),
            dma((devices,)),
            dma((chips,)),
            dma((devices,)),
            dma((devices, heads)),
            dma((devices, heads)),
            dma((devices, heads)),
            dma((devices, heads)),
        ],
        compiler_params=pltpu.CompilerParams(
            collective_id=0, has_side_effects=True, vmem_limit_bytes=56 * 1024 * 1024
        ),
    )(queries, latents, w_key, w_value)


def layout_of(mesh):
    group = list(mesh.devices.reshape(-1, mesh.shape["ctx"])[0])
    places = [tuple(d.coords) for d in group]
    chips = sorted(set(places))
    cores = len(group) // len(chips)
    varied = [axis for axis in range(3) if len({c[axis] for c in chips}) > 1]
    grid_y = 1
    if len(varied) == 2:
        fast = len({c[varied[0]] for c in chips})
        grid_y = 2 if fast == 2 else 1
    return grid_y, cores


def solution(mesh):
    grid_y, cores = layout_of(mesh)
    return jax.shard_map(
        functools.partial(on_device, grid_y, cores),
        mesh=mesh,
        in_specs=(
            P(("rep", "ctx"), None),
            P(("rep", "ctx"), None),
            P("ctx", None, None),
            P("ctx", None, None),
        ),
        out_specs=P(("rep", "ctx"), None),
        check_vma=False,
    )
```

```python
import functools
import math

import jax
import jax.numpy as jnp
from jax import lax
from jax.experimental import pallas as pl
from jax.experimental.pallas import tpu as pltpu
from jax.sharding import PartitionSpec as P

MESH = pl.DeviceIdType.MESH


def kernel(
    grid_y,
    cores,
    q_hbm,
    lat_hbm,
    wk_hbm,
    wv_hbm,
    o,
    q,
    lat,
    wkv,
    ropes,
    kv,
    load_sem,
    lat_recv,
    lat_send,
    lat_relay,
    kv_recv,
    kv_right,
    kv_left,
    kv_across,
):
    devices = kv.shape[0]
    heads = kv.shape[1]
    rows = kv.shape[3]
    nope = kv.shape[4]
    block = lat.shape[1]
    width = wkv.shape[1]
    rope = lat.shape[2] - width
    qk = nope + rope
    chips = devices // cores
    grid_z = chips // grid_y
    half = chips // 2
    scale = math.log2(math.e) / math.sqrt(qk)

    me = lax.axis_index("ctx")
    core = lax.rem(me, cores)
    my_chip = me // cores
    my_y = lax.rem(my_chip, grid_y)
    my_z = my_chip // grid_y
    place = (1 - my_y) * my_z + my_y * (2 * grid_z - 1 - my_z)

    def device_at(spot, which):
        spot = lax.rem(spot + 2 * chips, chips)
        y = spot // grid_z
        z = (1 - y) * spot + y * (2 * grid_z - 1 - spot)
        return (z * grid_y + y) * cores + which

    other_core = cores - 1 - core
    across = my_chip * cores + other_core
    right = device_at(place + 1, core)
    left = device_at(place - 1, core)

    q_copy = pltpu.make_async_copy(q_hbm, q, load_sem.at[0])
    lat_copy = pltpu.make_async_copy(lat_hbm, lat.at[me], load_sem.at[1])
    lat_copy.start()
    w_copies = []
    for j in range(heads):
        w_copies.append(
            pltpu.make_async_copy(wk_hbm.at[j], wkv.at[j, :, pl.ds(0, nope)], load_sem.at[2 + 2 * j])
        )
        w_copies.append(
            pltpu.make_async_copy(wv_hbm.at[j], wkv.at[j, :, pl.ds(nope, nope)], load_sem.at[3 + 2 * j])
        )
    for copy in w_copies:
        copy.start()
    q_copy.start()

    barrier = pltpu.get_barrier_semaphore()

    @pl.loop(1, chips)
    def _(d):
        pl.semaphore_signal(
            barrier, inc=1, device_id={"ctx": device_at(place + d, core)}, device_id_type=MESH
        )

    pl.semaphore_signal(barrier, inc=1, device_id={"ctx": across}, device_id_type=MESH)
    pl.semaphore_wait(barrier, chips)

    def lat_out(d):
        return pltpu.make_async_remote_copy(
            src_ref=lat_hbm,
            dst_ref=lat.at[me],
            send_sem=lat_send.at[d],
            recv_sem=lat_recv.at[me],
            device_id={"ctx": device_at(place + d, core)},
            device_id_type=MESH,
        )

    def lat_on(owner):
        return pltpu.make_async_remote_copy(
            src_ref=lat.at[owner],
            dst_ref=lat.at[owner],
            send_sem=lat_relay.at[owner],
            recv_sem=lat_recv.at[owner],
            device_id={"ctx": across},
            device_id_type=MESH,
        )

    @pl.loop(1, chips)
    def _(d):
        lat_out(chips - d).start()

    lat_copy.wait()
    lat_on(me).start()

    @pl.loop(1, chips)
    def _(d):
        owner = device_at(place + d, core)
        lat_on(owner).wait_recv()
        lat_on(owner).start()

    @pl.loop(0, chips)
    def _(d):
        lat_on(device_at(place + d, other_core)).wait_recv()

    for copy in w_copies:
        copy.wait()

    lat_all = lat[...].reshape(rows, lat.shape[2])
    rope_part = lat_all[:, width:]
    blank = jnp.zeros_like(rope_part)
    ropes[0] = jnp.concatenate([rope_part, blank], axis=1)
    ropes[1] = jnp.concatenate([blank, rope_part], axis=1)

    def parity(owner, j):
        if heads % 2 == 0:
            return j % 2
        return lax.rem(owner * heads + j, 2)

    def send(owner, j, sems, target):
        return pltpu.make_async_remote_copy(
            src_ref=kv.at[owner, j],
            dst_ref=kv.at[owner, j],
            send_sem=sems.at[owner, j],
            recv_sem=kv_recv.at[owner, j],
            device_id={"ctx": target},
            device_id_type=MESH,
        )

    def go_right(owner, j):
        return send(owner, j, kv_right, right)

    def go_left(owner, j):
        return send(owner, j, kv_left, left)

    def go_across(owner, j):
        return send(owner, j, kv_across, across)

    half_right = (heads + 1) // 2
    for j in range(heads + 1):
        if j < heads:
            both = jnp.dot(lat_all[:, :width], wkv[j], preferred_element_type=jnp.float32)
            keys = both[:, :nope]
            odd = parity(me, j)
            turned = jnp.concatenate([keys[:, rope:], keys[:, :rope]], axis=1)
            if isinstance(odd, int):
                keys = turned if odd else keys
            else:
                keys = jnp.where(odd == 1, turned, keys)
            kv[me, j, 0] = keys.astype(jnp.bfloat16)
            kv[me, j, 1] = both[:, nope:].astype(jnp.bfloat16)
        if j > 0:
            go_right(me, j - 1).start()
            go_left(me, j - 1).start()
            go_across(me, j - 1).start()

    q_copy.wait()

    lane = lax.broadcasted_iota(jnp.int32, (rows, nope), 1)
    upper = lane >= rope

    def attend(owner, j):
        odd = parity(owner, j)
        head = owner * heads + j
        pair = owner * (heads // 2) + j // 2 if heads % 2 == 0 else head // 2
        start = pl.multiple_of(pair * (2 * qk) + odd * nope, nope)
        queries = q[:, pl.ds(start, 2 * nope)]
        keys = kv[owner, j, 0]

        def even_keys():
            return jnp.concatenate([keys, ropes[0]], axis=1)

        def odd_keys():
            return jnp.concatenate(
                [jnp.where(upper, keys, jnp.zeros_like(keys)), jnp.where(upper, ropes[1], keys)], axis=1
            )

        if isinstance(odd, int):
            keys_full = odd_keys() if odd else even_keys()
        else:
            keys_full = jnp.where(odd == 1, odd_keys(), even_keys())
        scores = lax.dot_general(
            queries, keys_full, (((1,), (1,)), ((), ())), preferred_element_type=jnp.float32
        )
        row_max = jnp.max(scores, axis=1, keepdims=True)
        weights = jnp.exp2((scores - row_max) * scale)
        total = jnp.sum(weights, axis=1, keepdims=True)
        mixed = jnp.dot(weights.astype(jnp.bfloat16), kv[owner, j, 1], preferred_element_type=jnp.float32)
        o[:, pl.ds(pl.multiple_of(head * nope, nope), nope)] = (mixed * (1.0 / total)).astype(jnp.bfloat16)

    def attend_other(owners, js):
        for j in js:
            for owner in owners:
                go_across(owner, j).wait_recv()
            for owner in owners:
                attend(owner, j)

    for j in range(heads):
        attend(me, j)

    def ring_step(s, fwd_right, fwd_left, before):
        from_left = device_at(place - s, core)
        from_right = device_at(place + s, core)
        for j in range(heads):
            go_right(from_left, j).wait_recv()
            if j < fwd_right:
                go_right(from_left, j).start()
            go_across(from_left, j).start()
            go_left(from_right, j).wait_recv()
            if j >= fwd_left:
                go_left(from_right, j).start()
            go_across(from_right, j).start()
            for owner in before:
                go_across(owner, j).wait_recv()
            attend(from_left, j)
            attend(from_right, j)
            for owner in before:
                attend(owner, j)

    def others(s):
        return (device_at(place - s, other_core), device_at(place + s, other_core))

    if half > 1:
        first_right = heads if half > 2 else half_right
        first_left = 0 if half > 2 else half_right
        ring_step(1, first_right, first_left, (across,))
        if half > 3:

            @pl.loop(2, half - 1)
            def _(s):
                ring_step(s, heads, 0, others(s - 1))

        if half > 2:
            ring_step(half - 1, half_right, half_right, others(half - 2))

    far = device_at(place + half, core)
    far_other = device_at(place + half, other_core)
    last_before = others(half - 1) if half > 1 else (across,)
    order = []
    for j in range(half_right):
        order.append(j)
        if j + half_right < heads:
            order.append(j + half_right)
    for j in order:
        (go_right if j < half_right else go_left)(far, j).wait_recv()
        go_across(far, j).start()
        for owner in last_before:
            go_across(owner, j).wait_recv()
        for owner in last_before:
            attend(owner, j)
        attend(far, j)
    attend_other((far_other,), order)

    @pl.loop(1, chips)
    def _(d):
        lat_out(d).wait_send()

    @pl.loop(0, chips)
    def _(d):
        owner = device_at(place + d, core)
        lat_on(owner).wait_send()
        for j in range(heads):
            go_across(owner, j).wait_send()

    @pl.loop(0, half - 1)
    def _(s):
        for j in range(heads):
            go_right(device_at(place - s, core), j).wait_send()
            go_left(device_at(place + s, core), j).wait_send()

    for j in range(heads):
        if j < half_right:
            go_right(device_at(place - (half - 1), core), j).wait_send()
        else:
            go_left(device_at(place + (half - 1), core), j).wait_send()


def on_device(grid_y, cores, queries, latents, w_key, w_value):
    devices = lax.axis_size("ctx")
    heads, width, nope = w_key.shape
    query_rows = queries.shape[0]
    block = latents.shape[0]
    rows = block * devices
    chips = devices // cores
    anywhere = pl.BlockSpec(memory_space=pl.ANY)
    dma = pltpu.SemaphoreType.DMA
    return pl.pallas_call(
        functools.partial(kernel, grid_y, cores),
        out_shape=jax.ShapeDtypeStruct((query_rows, devices * heads * nope), jnp.bfloat16),
        in_specs=[anywhere] * 4,
        out_specs=pl.BlockSpec(memory_space=pltpu.VMEM),
        scratch_shapes=[
            pltpu.VMEM(queries.shape, jnp.bfloat16),
            pltpu.VMEM((devices, block, latents.shape[1]), jnp.bfloat16),
            pltpu.VMEM((heads, width, 2 * nope), jnp.bfloat16),
            pltpu.VMEM((2, rows, nope), jnp.bfloat16),
            pltpu.VMEM((devices, heads, 2, rows, nope), jnp.bfloat16),
            dma((2 + 2 * heads,)),
            dma((devices,)),
            dma((chips,)),
            dma((devices,)),
            dma((devices, heads)),
            dma((devices, heads)),
            dma((devices, heads)),
            dma((devices, heads)),
        ],
        compiler_params=pltpu.CompilerParams(
            collective_id=0, has_side_effects=True, vmem_limit_bytes=50 * 1024 * 1024
        ),
    )(queries, latents, w_key, w_value)


def layout_of(mesh):
    group = list(mesh.devices.reshape(-1, mesh.shape["ctx"])[0])
    places = [tuple(d.coords) for d in group]
    chips = sorted(set(places))
    cores = len(group) // len(chips)
    varied = [axis for axis in range(3) if len({c[axis] for c in chips}) > 1]
    grid_y = 1
    if len(varied) == 2:
        fast = len({c[varied[0]] for c in chips})
        grid_y = 2 if fast == 2 else 1
    return grid_y, cores


def solution(mesh):
    grid_y, cores = layout_of(mesh)
    return jax.shard_map(
        functools.partial(on_device, grid_y, cores),
        mesh=mesh,
        in_specs=(
            P(("rep", "ctx"), None),
            P(("rep", "ctx"), None),
            P("ctx", None, None),
            P("ctx", None, None),
        ),
        out_specs=P(("rep", "ctx"), None),
        check_vma=False,
    )
```

```python
import functools
import math

import jax
import jax.numpy as jnp
from jax import lax
from jax.experimental import pallas as pl
from jax.experimental.pallas import tpu as pltpu
from jax.sharding import PartitionSpec as P

MESH = pl.DeviceIdType.MESH


def kernel(
    grid_y,
    cores,
    q_hbm,
    lat_hbm,
    wk_hbm,
    wv_hbm,
    o,
    q,
    lat,
    wkv,
    ropes,
    kv,
    load_sem,
    lat_recv,
    lat_send,
    lat_relay,
    kv_recv,
    kv_right,
    kv_left,
    kv_across,
):
    devices = kv.shape[0]
    heads = kv.shape[1]
    rows = 2 * kv.shape[4]
    nope = kv.shape[5]
    block = lat.shape[1]
    width = wkv.shape[1]
    rope = lat.shape[2] - width
    qk = nope + rope
    chips = devices // cores
    grid_z = chips // grid_y
    half = chips // 2
    scale = math.log2(math.e) / math.sqrt(qk)

    me = lax.axis_index("ctx")
    core = lax.rem(me, cores)
    my_chip = me // cores
    my_y = lax.rem(my_chip, grid_y)
    my_z = my_chip // grid_y
    place = (1 - my_y) * my_z + my_y * (2 * grid_z - 1 - my_z)

    def device_at(spot, which):
        spot = lax.rem(spot + 2 * chips, chips)
        y = spot // grid_z
        z = (1 - y) * spot + y * (2 * grid_z - 1 - spot)
        return (z * grid_y + y) * cores + which

    other_core = cores - 1 - core
    across = my_chip * cores + other_core
    right = device_at(place + 1, core)
    left = device_at(place - 1, core)

    q_copy = pltpu.make_async_copy(q_hbm, q, load_sem.at[0])
    lat_copy = pltpu.make_async_copy(lat_hbm, lat.at[me], load_sem.at[1])
    lat_copy.start()
    w_copies = []
    for j in range(heads):
        w_copies.append(
            pltpu.make_async_copy(wk_hbm.at[j], wkv.at[j, :, pl.ds(0, nope)], load_sem.at[2 + 2 * j])
        )
        w_copies.append(
            pltpu.make_async_copy(wv_hbm.at[j], wkv.at[j, :, pl.ds(nope, nope)], load_sem.at[3 + 2 * j])
        )
    for copy in w_copies:
        copy.start()
    q_copy.start()

    barrier = pltpu.get_barrier_semaphore()

    @pl.loop(1, chips)
    def _(d):
        pl.semaphore_signal(
            barrier, inc=1, device_id={"ctx": device_at(place + d, core)}, device_id_type=MESH
        )

    pl.semaphore_signal(barrier, inc=1, device_id={"ctx": across}, device_id_type=MESH)
    pl.semaphore_wait(barrier, chips)

    near = me // (devices // 2)
    chips_half = chips // 2

    def near_chip(i):
        return near * chips_half + lax.rem(my_chip - near * chips_half + i, chips_half)

    def far_chip(i):
        return (1 - near) * chips_half + lax.rem(my_chip - near * chips_half + i, chips_half)

    def lat_out(chip):
        return pltpu.make_async_remote_copy(
            src_ref=lat_hbm,
            dst_ref=lat.at[me],
            send_sem=lat_send.at[chip],
            recv_sem=lat_recv.at[me],
            device_id={"ctx": chip * cores + core},
            device_id_type=MESH,
        )

    def lat_on(owner):
        return pltpu.make_async_remote_copy(
            src_ref=lat.at[owner],
            dst_ref=lat.at[owner],
            send_sem=lat_relay.at[owner],
            recv_sem=lat_recv.at[owner],
            device_id={"ctx": across},
            device_id_type=MESH,
        )

    @pl.loop(1, chips_half)
    def _(i):
        lat_out(near_chip(i)).start()

    @pl.loop(0, chips_half)
    def _(i):
        lat_out(far_chip(i)).start()

    lat_copy.wait()
    lat_on(me).start()

    def relay(chip):
        owner = chip * cores + core
        lat_on(owner).wait_recv()
        lat_on(owner).start()

    @pl.loop(1, chips_half)
    def _(i):
        relay(near_chip(i))

    @pl.loop(0, chips_half)
    def _(i):
        lat_on(near_chip(i) * cores + other_core).wait_recv()

    for copy in w_copies:
        copy.wait()

    def parity(owner, j):
        if heads % 2 == 0:
            return j % 2
        return lax.rem(owner * heads + j, 2)

    def send(owner, j, part, sems, target):
        return pltpu.make_async_remote_copy(
            src_ref=kv.at[owner, j, part],
            dst_ref=kv.at[owner, j, part],
            send_sem=sems.at[owner, j, part],
            recv_sem=kv_recv.at[owner, j, part],
            device_id={"ctx": target},
            device_id_type=MESH,
        )

    def first_part(owner):
        return owner // (devices // 2)

    def go_right(owner, j, part):
        return send(owner, j, part, kv_right, right)

    def go_left(owner, j, part):
        return send(owner, j, part, kv_left, left)

    def go_across(owner, j):
        return pltpu.make_async_remote_copy(
            src_ref=kv.at[owner, j],
            dst_ref=kv.at[owner, j],
            send_sem=kv_across.at[owner, j],
            recv_sem=kv_recv.at[owner, j, 0],
            device_id={"ctx": across},
            device_id_type=MESH,
        )

    half_right = (heads + 1) // 2

    def project(part, last):
        some = lat[pl.ds(part * (devices // 2), devices // 2)].reshape(rows // 2, lat.shape[2])
        for j in range(heads + 1):
            if j < heads:
                both = jnp.dot(some[:, :width], wkv[j], preferred_element_type=jnp.float32)
                keys = both[:, :nope]
                odd = parity(me, j)
                turned = jnp.concatenate([keys[:, rope:], keys[:, :rope]], axis=1)
                if isinstance(odd, int):
                    keys = turned if odd else keys
                else:
                    keys = jnp.where(odd == 1, turned, keys)
                kv[me, j, part, 0] = keys.astype(jnp.bfloat16)
                kv[me, j, part, 1] = both[:, nope:].astype(jnp.bfloat16)
            if j > 0:
                go_right(me, j - 1, part).start()
                go_left(me, j - 1, part).start()
                if last:
                    go_across(me, j - 1).start()

    project(near, False)

    @pl.loop(0, chips_half)
    def _(i):
        relay(far_chip(i))

    @pl.loop(0, chips_half)
    def _(i):
        lat_on(far_chip(i) * cores + other_core).wait_recv()

    project(1 - near, True)

    rope_part = lat[...].reshape(rows, lat.shape[2])[:, width:]
    blank = jnp.zeros_like(rope_part)
    ropes[0] = jnp.concatenate([rope_part, blank], axis=1)
    ropes[1] = jnp.concatenate([blank, rope_part], axis=1)

    q_copy.wait()

    lane = lax.broadcasted_iota(jnp.int32, (rows, nope), 1)
    upper = lane >= rope

    def attend(owner, j):
        odd = parity(owner, j)
        head = owner * heads + j
        pair = owner * (heads // 2) + j // 2 if heads % 2 == 0 else head // 2
        start = pl.multiple_of(pair * (2 * qk) + odd * nope, nope)
        queries = q[:, pl.ds(start, 2 * nope)]
        keys = kv[owner, j, :, 0].reshape(rows, nope)
        values = kv[owner, j, :, 1].reshape(rows, nope)

        def even_keys():
            return jnp.concatenate([keys, ropes[0]], axis=1)

        def odd_keys():
            return jnp.concatenate(
                [jnp.where(upper, keys, jnp.zeros_like(keys)), jnp.where(upper, ropes[1], keys)], axis=1
            )

        if isinstance(odd, int):
            keys_full = odd_keys() if odd else even_keys()
        else:
            keys_full = jnp.where(odd == 1, odd_keys(), even_keys())
        scores = lax.dot_general(
            queries, keys_full, (((1,), (1,)), ((), ())), preferred_element_type=jnp.float32
        )
        row_max = jnp.max(scores, axis=1, keepdims=True)
        weights = jnp.exp2((scores - row_max) * scale)
        total = jnp.sum(weights, axis=1, keepdims=True)
        mixed = jnp.dot(weights.astype(jnp.bfloat16), values, preferred_element_type=jnp.float32)
        o[:, pl.ds(pl.multiple_of(head * nope, nope), nope)] = (mixed * (1.0 / total)).astype(jnp.bfloat16)

    def attend_other(owners, js):
        for j in js:
            for owner in owners:
                go_across(owner, j).wait_recv()
            for owner in owners:
                attend(owner, j)

    for j in range(heads):
        attend(me, j)

    def ring_step(s, fwd_right, fwd_left, before):
        from_left = device_at(place - s, core)
        from_right = device_at(place + s, core)
        for turn in range(2):
            part_l = first_part(from_left) if turn == 0 else 1 - first_part(from_left)
            part_r = first_part(from_right) if turn == 0 else 1 - first_part(from_right)
            for j in range(heads):
                go_right(from_left, j, part_l).wait_recv()
                if j < fwd_right:
                    go_right(from_left, j, part_l).start()
                go_left(from_right, j, part_r).wait_recv()
                if j >= fwd_left:
                    go_left(from_right, j, part_r).start()
                if turn == 0:
                    for owner in before:
                        go_across(owner, j).wait_recv()
                    for owner in before:
                        attend(owner, j)
                else:
                    go_across(from_left, j).start()
                    go_across(from_right, j).start()
                    attend(from_left, j)
                    attend(from_right, j)

    def others(s):
        return (device_at(place - s, other_core), device_at(place + s, other_core))

    if half > 1:
        first_right = heads if half > 2 else half_right
        first_left = 0 if half > 2 else half_right
        ring_step(1, first_right, first_left, (across,))
        if half > 3:

            @pl.loop(2, half - 1)
            def _(s):
                ring_step(s, heads, 0, others(s - 1))

        if half > 2:
            ring_step(half - 1, half_right, half_right, others(half - 2))

    far = device_at(place + half, core)
    far_other = device_at(place + half, other_core)
    last_before = others(half - 1) if half > 1 else (across,)
    order = []
    for j in range(half_right):
        order.append(j)
        if j + half_right < heads:
            order.append(j + half_right)
    for j in order:
        (go_right if j < half_right else go_left)(far, j, first_part(far)).wait_recv()
        for owner in last_before:
            go_across(owner, j).wait_recv()
        for owner in last_before:
            attend(owner, j)
    for j in order:
        (go_right if j < half_right else go_left)(far, j, 1 - first_part(far)).wait_recv()
        go_across(far, j).start()
        attend(far, j)
    attend_other((far_other,), order)

    @pl.loop(1, chips_half)
    def _(i):
        lat_out(near_chip(i)).wait_send()

    @pl.loop(0, chips_half)
    def _(i):
        lat_out(far_chip(i)).wait_send()

    @pl.loop(0, chips)
    def _(d):
        owner = device_at(place + d, core)
        lat_on(owner).wait_send()
        for j in range(heads):
            go_across(owner, j).wait_send()

    @pl.loop(0, half - 1)
    def _(s):
        for j in range(heads):
            for part in range(2):
                go_right(device_at(place - s, core), j, part).wait_send()
                go_left(device_at(place + s, core), j, part).wait_send()

    for j in range(heads):
        for part in range(2):
            if j < half_right:
                go_right(device_at(place - (half - 1), core), j, part).wait_send()
            else:
                go_left(device_at(place + (half - 1), core), j, part).wait_send()


def on_device(grid_y, cores, queries, latents, w_key, w_value):
    devices = lax.axis_size("ctx")
    heads, width, nope = w_key.shape
    query_rows = queries.shape[0]
    block = latents.shape[0]
    rows = block * devices
    chips = devices // cores
    anywhere = pl.BlockSpec(memory_space=pl.ANY)
    dma = pltpu.SemaphoreType.DMA
    return pl.pallas_call(
        functools.partial(kernel, grid_y, cores),
        out_shape=jax.ShapeDtypeStruct((query_rows, devices * heads * nope), jnp.bfloat16),
        in_specs=[anywhere] * 4,
        out_specs=pl.BlockSpec(memory_space=pltpu.VMEM),
        scratch_shapes=[
            pltpu.VMEM(queries.shape, jnp.bfloat16),
            pltpu.VMEM((devices, block, latents.shape[1]), jnp.bfloat16),
            pltpu.VMEM((heads, width, 2 * nope), jnp.bfloat16),
            pltpu.VMEM((2, rows, nope), jnp.bfloat16),
            pltpu.VMEM((devices, heads, 2, 2, rows // 2, nope), jnp.bfloat16),
            dma((2 + 2 * heads,)),
            dma((devices,)),
            dma((chips,)),
            dma((devices,)),
            dma((devices, heads, 2)),
            dma((devices, heads, 2)),
            dma((devices, heads, 2)),
            dma((devices, heads)),
        ],
        compiler_params=pltpu.CompilerParams(
            collective_id=0, has_side_effects=True, vmem_limit_bytes=50 * 1024 * 1024
        ),
    )(*(pltpu.with_memory_space_constraint(a, pltpu.HBM) for a in (queries, latents, w_key, w_value)))


def layout_of(mesh):
    group = list(mesh.devices.reshape(-1, mesh.shape["ctx"])[0])
    places = [tuple(d.coords) for d in group]
    chips = sorted(set(places))
    cores = len(group) // len(chips)
    varied = [axis for axis in range(3) if len({c[axis] for c in chips}) > 1]
    grid_y = 1
    if len(varied) == 2:
        fast = len({c[varied[0]] for c in chips})
        grid_y = 2 if fast == 2 else 1
    return grid_y, cores


def solution(mesh):
    grid_y, cores = layout_of(mesh)
    return jax.shard_map(
        functools.partial(on_device, grid_y, cores),
        mesh=mesh,
        in_specs=(
            P(("rep", "ctx"), None),
            P(("rep", "ctx"), None),
            P("ctx", None, None),
            P("ctx", None, None),
        ),
        out_specs=P(("rep", "ctx"), None),
        check_vma=False,
    )
```

```python
import functools
import math

import jax
import jax.numpy as jnp
from jax import lax
from jax.experimental import pallas as pl
from jax.experimental.pallas import tpu as pltpu
from jax.sharding import PartitionSpec as P

MESH = pl.DeviceIdType.MESH


def kernel(
    grid_y,
    cores,
    q_hbm,
    lat_hbm,
    wk_hbm,
    wv_hbm,
    o,
    q,
    lat,
    wkv,
    ropes,
    kv,
    load_sem,
    lat_recv,
    lat_send,
    lat_relay,
    kv_recv,
    kv_right,
    kv_left,
    kv_across,
):
    devices = kv.shape[0]
    heads = kv.shape[1]
    rows = 2 * kv.shape[4]
    nope = kv.shape[5]
    block = lat.shape[1]
    width = wkv.shape[1]
    rope = lat.shape[2] - width
    qk = nope + rope
    chips = devices // cores
    grid_z = chips // grid_y
    half = chips // 2
    scale = math.log2(math.e) / math.sqrt(qk)

    me = lax.axis_index("ctx")
    core = lax.rem(me, cores)
    my_chip = me // cores
    my_y = lax.rem(my_chip, grid_y)
    my_z = my_chip // grid_y
    place = (1 - my_y) * my_z + my_y * (2 * grid_z - 1 - my_z)

    def device_at(spot, which):
        spot = lax.rem(spot + 2 * chips, chips)
        y = spot // grid_z
        z = (1 - y) * spot + y * (2 * grid_z - 1 - spot)
        return (z * grid_y + y) * cores + which

    other_core = cores - 1 - core
    across = my_chip * cores + other_core
    right = device_at(place + 1, core)
    left = device_at(place - 1, core)

    q_copy = pltpu.make_async_copy(q_hbm, q, load_sem.at[0])
    lat_copy = pltpu.make_async_copy(lat_hbm, lat.at[me], load_sem.at[1])
    lat_copy.start()
    w_copies = []
    for j in range(heads):
        w_copies.append(
            pltpu.make_async_copy(wk_hbm.at[j], wkv.at[j, :, pl.ds(0, nope)], load_sem.at[2 + 2 * j])
        )
        w_copies.append(
            pltpu.make_async_copy(wv_hbm.at[j], wkv.at[j, :, pl.ds(nope, nope)], load_sem.at[3 + 2 * j])
        )
    for copy in w_copies:
        copy.start()

    barrier = pltpu.get_barrier_semaphore()

    @pl.loop(1, chips)
    def _(d):
        pl.semaphore_signal(
            barrier, inc=1, device_id={"ctx": device_at(place + d, core)}, device_id_type=MESH
        )

    pl.semaphore_signal(barrier, inc=1, device_id={"ctx": across}, device_id_type=MESH)
    pl.semaphore_wait(barrier, chips)

    near = me // (devices // 2)
    chips_half = chips // 2

    def near_chip(i):
        return near * chips_half + lax.rem(my_chip - near * chips_half + i, chips_half)

    def far_chip(i):
        return (1 - near) * chips_half + lax.rem(my_chip - near * chips_half + i, chips_half)

    def lat_out(chip):
        return pltpu.make_async_remote_copy(
            src_ref=lat_hbm,
            dst_ref=lat.at[me],
            send_sem=lat_send.at[chip],
            recv_sem=lat_recv.at[me],
            device_id={"ctx": chip * cores + core},
            device_id_type=MESH,
        )

    def lat_on(owner):
        return pltpu.make_async_remote_copy(
            src_ref=lat.at[owner],
            dst_ref=lat.at[owner],
            send_sem=lat_relay.at[owner],
            recv_sem=lat_recv.at[owner],
            device_id={"ctx": across},
            device_id_type=MESH,
        )

    @pl.loop(1, chips_half)
    def _(i):
        lat_out(near_chip(i)).start()

    @pl.loop(0, chips_half)
    def _(i):
        lat_out(far_chip(i)).start()

    lat_copy.wait()
    lat_on(me).start()

    def relay(chip):
        owner = chip * cores + core
        lat_on(owner).wait_recv()
        lat_on(owner).start()

    @pl.loop(1, chips_half)
    def _(i):
        relay(near_chip(i))

    @pl.loop(0, chips_half)
    def _(i):
        lat_on(near_chip(i) * cores + other_core).wait_recv()

    for copy in w_copies:
        copy.wait()

    def parity(owner, j):
        if heads % 2 == 0:
            return j % 2
        return lax.rem(owner * heads + j, 2)

    def send(owner, j, part, sems, target):
        return pltpu.make_async_remote_copy(
            src_ref=kv.at[owner, j, part],
            dst_ref=kv.at[owner, j, part],
            send_sem=sems.at[owner, j, part],
            recv_sem=kv_recv.at[owner, j, part],
            device_id={"ctx": target},
            device_id_type=MESH,
        )

    def first_part(owner):
        return owner // (devices // 2)

    def go_right(owner, j, part):
        return send(owner, j, part, kv_right, right)

    def go_left(owner, j, part):
        return send(owner, j, part, kv_left, left)

    def go_across(owner, j):
        return pltpu.make_async_remote_copy(
            src_ref=kv.at[owner, j],
            dst_ref=kv.at[owner, j],
            send_sem=kv_across.at[owner, j],
            recv_sem=kv_recv.at[owner, j, 0],
            device_id={"ctx": across},
            device_id_type=MESH,
        )

    half_right = (heads + 1) // 2

    def project(part, last):
        some = lat[pl.ds(part * (devices // 2), devices // 2)].reshape(rows // 2, lat.shape[2])
        for j in range(heads + 1):
            if j < heads:
                both = jnp.dot(some[:, :width], wkv[j], preferred_element_type=jnp.float32)
                keys = both[:, :nope]
                odd = parity(me, j)
                turned = jnp.concatenate([keys[:, rope:], keys[:, :rope]], axis=1)
                if isinstance(odd, int):
                    keys = turned if odd else keys
                else:
                    keys = jnp.where(odd == 1, turned, keys)
                kv[me, j, part, 0] = keys.astype(jnp.bfloat16)
                kv[me, j, part, 1] = both[:, nope:].astype(jnp.bfloat16)
            if j > 0:
                go_right(me, j - 1, part).start()
                go_left(me, j - 1, part).start()
                if last:
                    go_across(me, j - 1).start()

    project(near, False)
    q_copy.start()

    @pl.loop(0, chips_half)
    def _(i):
        relay(far_chip(i))

    @pl.loop(0, chips_half)
    def _(i):
        lat_on(far_chip(i) * cores + other_core).wait_recv()

    project(1 - near, True)

    rope_part = lat[...].reshape(rows, lat.shape[2])[:, width:]
    blank = jnp.zeros_like(rope_part)
    ropes[0] = jnp.concatenate([rope_part, blank], axis=1)
    ropes[1] = jnp.concatenate([blank, rope_part], axis=1)

    q_copy.wait()

    lane = lax.broadcasted_iota(jnp.int32, (rows, nope), 1)
    upper = lane >= rope

    def attend(owner, j):
        odd = parity(owner, j)
        head = owner * heads + j
        pair = owner * (heads // 2) + j // 2 if heads % 2 == 0 else head // 2
        start = pl.multiple_of(pair * (2 * qk) + odd * nope, nope)
        queries = q[:, pl.ds(start, 2 * nope)]
        keys = kv[owner, j, :, 0].reshape(rows, nope)
        values = kv[owner, j, :, 1].reshape(rows, nope)

        def even_keys():
            return jnp.concatenate([keys, ropes[0]], axis=1)

        def odd_keys():
            return jnp.concatenate(
                [jnp.where(upper, keys, jnp.zeros_like(keys)), jnp.where(upper, ropes[1], keys)], axis=1
            )

        if isinstance(odd, int):
            keys_full = odd_keys() if odd else even_keys()
        else:
            keys_full = jnp.where(odd == 1, odd_keys(), even_keys())
        scores = lax.dot_general(
            queries, keys_full, (((1,), (1,)), ((), ())), preferred_element_type=jnp.float32
        )
        row_max = jnp.max(scores, axis=1, keepdims=True)
        weights = jnp.exp2((scores - row_max) * scale)
        total = jnp.sum(weights, axis=1, keepdims=True)
        mixed = jnp.dot(weights.astype(jnp.bfloat16), values, preferred_element_type=jnp.float32)
        o[:, pl.ds(pl.multiple_of(head * nope, nope), nope)] = (mixed * (1.0 / total)).astype(jnp.bfloat16)

    for j in range(heads):
        attend(me, j)

    def ring_step(s, fwd_right, fwd_left, before):
        from_left = device_at(place - s, core)
        from_right = device_at(place + s, core)
        for turn in range(2):
            part_l = first_part(from_left) if turn == 0 else 1 - first_part(from_left)
            part_r = first_part(from_right) if turn == 0 else 1 - first_part(from_right)
            for j in range(heads):
                go_right(from_left, j, part_l).wait_recv()
                if j < fwd_right:
                    go_right(from_left, j, part_l).start()
                go_left(from_right, j, part_r).wait_recv()
                if j >= fwd_left:
                    go_left(from_right, j, part_r).start()
                if turn == 0:
                    for owner in before:
                        go_across(owner, j).wait_recv()
                    for owner in before:
                        attend(owner, j)
                else:
                    go_across(from_left, j).start()
                    go_across(from_right, j).start()
                    attend(from_left, j)
                    attend(from_right, j)

    def others(s):
        return (device_at(place - s, other_core), device_at(place + s, other_core))

    if half > 1:
        first_right = heads if half > 2 else half_right
        first_left = 0 if half > 2 else half_right
        ring_step(1, first_right, first_left, (across,))
        if half > 3:

            @pl.loop(2, half - 1)
            def _(s):
                ring_step(s, heads, 0, others(s - 1))

        if half > 2:
            ring_step(half - 1, half_right, half_right, others(half - 2))

    far = device_at(place + half, core)
    far_other = device_at(place + half, other_core)
    last_before = others(half - 1) if half > 1 else (across,)
    order = []
    for j in range(half_right):
        order.append(j)
        if j + half_right < heads:
            order.append(j + half_right)
    for j in order:
        (go_right if j < half_right else go_left)(far, j, first_part(far)).wait_recv()
        send(far, j, first_part(far), kv_right, across).start()
        for owner in last_before:
            go_across(owner, j).wait_recv()
        for owner in last_before:
            attend(owner, j)
    for j in order:
        (go_right if j < half_right else go_left)(far, j, 1 - first_part(far)).wait_recv()
        send(far, j, 1 - first_part(far), kv_right, across).start()
        attend(far, j)
    for j in order:
        for part in range(2):
            send(far_other, j, part, kv_right, across).wait_recv()
        attend(far_other, j)

    @pl.loop(1, chips_half)
    def _(i):
        lat_out(near_chip(i)).wait_send()

    @pl.loop(0, chips_half)
    def _(i):
        lat_out(far_chip(i)).wait_send()

    @pl.loop(0, chips)
    def _(d):
        owner = device_at(place + d, core)
        lat_on(owner).wait_send()

    @pl.loop(half + 1, chips + half)
    def _(d):
        for j in range(heads):
            go_across(device_at(place + d, core), j).wait_send()

    for j in range(heads):
        for part in range(2):
            send(far, j, part, kv_right, across).wait_send()

    @pl.loop(0, half - 1)
    def _(s):
        for j in range(heads):
            for part in range(2):
                go_right(device_at(place - s, core), j, part).wait_send()
                go_left(device_at(place + s, core), j, part).wait_send()

    for j in range(heads):
        for part in range(2):
            if j < half_right:
                go_right(device_at(place - (half - 1), core), j, part).wait_send()
            else:
                go_left(device_at(place + (half - 1), core), j, part).wait_send()


def on_device(grid_y, cores, queries, latents, w_key, w_value):
    devices = lax.axis_size("ctx")
    heads, width, nope = w_key.shape
    query_rows = queries.shape[0]
    block = latents.shape[0]
    rows = block * devices
    chips = devices // cores
    anywhere = pl.BlockSpec(memory_space=pl.ANY)
    dma = pltpu.SemaphoreType.DMA
    return pl.pallas_call(
        functools.partial(kernel, grid_y, cores),
        out_shape=jax.ShapeDtypeStruct((query_rows, devices * heads * nope), jnp.bfloat16),
        in_specs=[anywhere] * 4,
        out_specs=pl.BlockSpec(memory_space=pltpu.VMEM),
        scratch_shapes=[
            pltpu.VMEM(queries.shape, jnp.bfloat16),
            pltpu.VMEM((devices, block, latents.shape[1]), jnp.bfloat16),
            pltpu.VMEM((heads, width, 2 * nope), jnp.bfloat16),
            pltpu.VMEM((2, rows, nope), jnp.bfloat16),
            pltpu.VMEM((devices, heads, 2, 2, rows // 2, nope), jnp.bfloat16),
            dma((2 + 2 * heads,)),
            dma((devices,)),
            dma((chips,)),
            dma((devices,)),
            dma((devices, heads, 2)),
            dma((devices, heads, 2)),
            dma((devices, heads, 2)),
            dma((devices, heads)),
        ],
        compiler_params=pltpu.CompilerParams(
            collective_id=0, has_side_effects=True, vmem_limit_bytes=50 * 1024 * 1024
        ),
    )(*(pltpu.with_memory_space_constraint(a, pltpu.HBM) for a in (queries, latents, w_key, w_value)))


def layout_of(mesh):
    group = list(mesh.devices.reshape(-1, mesh.shape["ctx"])[0])
    places = [tuple(d.coords) for d in group]
    chips = sorted(set(places))
    cores = len(group) // len(chips)
    varied = [axis for axis in range(3) if len({c[axis] for c in chips}) > 1]
    grid_y = 1
    if len(varied) == 2:
        fast = len({c[varied[0]] for c in chips})
        grid_y = 2 if fast == 2 else 1
    return grid_y, cores


def solution(mesh):
    grid_y, cores = layout_of(mesh)
    return jax.shard_map(
        functools.partial(on_device, grid_y, cores),
        mesh=mesh,
        in_specs=(
            P(("rep", "ctx"), None),
            P(("rep", "ctx"), None),
            P("ctx", None, None),
            P("ctx", None, None),
        ),
        out_specs=P(("rep", "ctx"), None),
        check_vma=False,
    )
```
